512 devices in a mesh: row: 16 (over z), col: 16 (over y, x), rep: 2 (over core).
Axes of the slice: x: 4, y: 4, z: 16, core: 2. Of those that a mesh axis runs over, the one named last changes fastest.
Arguments:
- tokens: bfloat16 [512, 4096], P(('col', 'rep'), 'row'), may hold values from -6 to 6
- grad_out: bfloat16 [512, 4096], P(('col', 'rep'), 'row'), may hold values from -2.5 to 2.5
- gate_weight: bfloat16 [4096, 14336], P('row', 'col'), may hold values from -0.09375 to 0.09375
- up_weight: bfloat16 [4096, 14336], P('row', 'col'), may hold values from -0.09375 to 0.09375
- down_weight: bfloat16 [14336, 4096], P('col', 'row'), may hold values from -0.046875 to 0.046875
- gate_keep: int32 [32, 112], P('row', 'col'), may hold values from 0 to 1, as said below
- up_keep: int32 [32, 112], P('row', 'col'), may hold values from 0 to 1, as said below
- down_keep: int32 [112, 32], P('col', 'row'), may hold values from 0 to 1, as said below
Outputs:
- mixed: bfloat16 [512, 4096], P(('col', 'rep'), 'row')
- input_grad: bfloat16 [512, 4096], P(('col', 'rep'), 'row')
- gate_weight_grad: bfloat16 [4096, 14336], P('row', 'col')
- up_weight_grad: bfloat16 [4096, 14336], P('row', 'col')
- down_weight_grad: bfloat16 [14336, 4096], P('col', 'row')
The draws below stay inside these ranges and needn't reach their ends.
Inputs may be any that keep to these rules, and one draw needn't show every extreme that they name: `gate_keep`: 1 keeps the 128 x 128 block of the gate projection, 0 prunes it; the kept share differs from one device's region to the next. `up_keep`: 1 keeps the 128 x 128 block of the up projection, 0 prunes it; the kept share differs from one device's region to the next. `down_keep`: 1 keeps the 128 x 128 block of the down projection, 0 prunes it; the kept share differs from one device's region to the next.
All inputs are finite; a program needn't handle non-finite values.
Results may differ from the reference program's by a relative error of at most 0.025.
Values may be sent and summed in bfloat16 or wider, within the bound.
No kernel may reach another device: no remote copies, remote signals or barrier semaphores. Data moves between devices by JAX's collectives and lax.ppermute only.
A program may use at most 64 MiB of HBM per device.

```python
import jax
import jax.numpy as jnp
from jax import lax

D = 4096
FF = 14336
BLOCK = 128
TOK_DEV = 16
TOKENS = 512
ROW_BLOCKS = 2
COL_BLOCKS = 7
N_ROW = 16
N_COL = 16
N_REP = 2


def keep_pattern(key, block_rows, block_cols, group_rows, group_cols):
    level_key, cell_key = jax.random.split(key)
    levels = jax.random.randint(level_key, (block_rows // group_rows, block_cols // group_cols), 1, 9)
    cells = jax.random.randint(cell_key, (block_rows, block_cols), 0, 8)
    spread = jnp.repeat(jnp.repeat(levels, group_rows, axis=0), group_cols, axis=1)
    return (cells < spread).astype(jnp.int32)


def draw_gate_keep(key, part):
    return keep_pattern(jax.random.fold_in(key, 11), D // BLOCK, FF // BLOCK, ROW_BLOCKS, COL_BLOCKS)


def draw_up_keep(key, part):
    return keep_pattern(jax.random.fold_in(key, 23), D // BLOCK, FF // BLOCK, ROW_BLOCKS, COL_BLOCKS)


def draw_down_keep(key, part):
    return keep_pattern(jax.random.fold_in(key, 37), FF // BLOCK, D // BLOCK, COL_BLOCKS, ROW_BLOCKS)


def block_scale(own_key, shape, pieces, low, high):
    gain, own = 1.0, jax.random.fold_in(own_key, 6)
    for dim, blocks in pieces:
        draws = jnp.exp(jax.random.uniform(jax.random.fold_in(own, dim), (blocks,), jnp.float32, low / len(pieces), high / len(pieces)))
        gain = gain * jnp.repeat(draws, shape[dim] // blocks).reshape([-1 if axis == dim else 1 for axis in range(len(shape))])
    return gain


def scatter_about(stream_key, extent, scale, most, cuts=(), kind=jnp.bfloat16):
    level = block_scale(stream_key, extent, cuts, -0.22, 0.18) if cuts else 1.0
    array = jax.random.normal(stream_key, extent, jnp.float32) * scale * level
    return jnp.minimum(jnp.maximum(array, -most), most).astype(kind)


def setup_inputs(seed: int = 0) -> dict:
    key_list = jax.random.split(jax.random.key(seed), 9)
    tokens = scatter_about(key_list[0], (TOKENS, D), 1.0, 6.0, ((0, 32), (1, 16)))
    grad_out = scatter_about(key_list[1], (TOKENS, D), 0.25, 2.5, ((0, 32), (1, 16)))
    gate_weight = scatter_about(key_list[2], (D, FF), D ** -0.5, 0.09375, ((0, 16), (1, 16)))
    up_weight = scatter_about(key_list[3], (D, FF), D ** -0.5, 0.09375, ((0, 16), (1, 16)))
    down_weight = scatter_about(key_list[4], (FF, D), FF ** -0.5, 0.046875, ((0, 16), (1, 16)))
    gate_keep = draw_gate_keep(jax.random.fold_in(key_list[8], 71), 0)
    up_keep = draw_up_keep(jax.random.fold_in(key_list[8], 71), 0)
    down_keep = draw_down_keep(jax.random.fold_in(key_list[8], 71), 0)
    return {"tokens": tokens, "grad_out": grad_out, "gate_weight": gate_weight, "up_weight": up_weight, "down_weight": down_weight, "gate_keep": gate_keep, "up_keep": up_keep, "down_keep": down_keep}


def masked(weight, keep):
    rows, cols = keep.shape
    tiled = weight.reshape(rows, weight.shape[0] // rows, cols, weight.shape[1] // cols)
    return (tiled * keep[:, None, :, None].astype(weight.dtype)).reshape(weight.shape)


def rounded(value):
    narrow = lax.optimization_barrier(value.astype(jnp.bfloat16))
    return narrow.astype(jnp.float32)


def block_sum(left, weight):
    size = left.shape[1] // N_ROW

    def step(total, index):
        begin = (index * size).astype(jnp.int32)
        part_left = lax.dynamic_slice_in_dim(left, begin, size, 1)
        part_weight = lax.dynamic_slice_in_dim(weight, begin, size, 0)
        partial_value = jnp.dot(part_left, part_weight, preferred_element_type=jnp.float32)
        return total + rounded(partial_value), None

    start_total = jnp.zeros((left.shape[0], weight.shape[1]), jnp.float32)
    total, unused = lax.scan(step, start_total, jnp.arange(N_ROW, dtype=jnp.int32))
    return total


def reference(tokens, grad_out, gate_weight, up_weight, down_weight, gate_keep, up_keep, down_keep):
    gate_eff = masked(gate_weight, gate_keep)
    up_eff = masked(up_weight, up_keep)
    down_eff = masked(down_weight, down_keep)
    token_groups = tokens.reshape(N_COL, N_REP, TOK_DEV, D)
    grad_groups = grad_out.reshape(N_COL, N_REP, TOK_DEV, D)
    mixed_list = []
    input_list = []
    gate_total = jnp.zeros((D, FF), jnp.float32)
    up_total = jnp.zeros((D, FF), jnp.float32)
    down_total = jnp.zeros((FF, D), jnp.float32)
    for replica in range(N_REP):
        x_rows = token_groups[:, replica].reshape(N_COL * TOK_DEV, D)
        dy_rows = grad_groups[:, replica].reshape(N_COL * TOK_DEV, D)
        gate_sum = block_sum(x_rows, gate_eff)
        up_sum = block_sum(x_rows, up_eff)
        gate_sig = jax.nn.sigmoid(gate_sum)
        hidden = (gate_sum * gate_sig * up_sum).astype(jnp.bfloat16)
        mixed = jnp.dot(hidden, down_eff, preferred_element_type=jnp.float32).astype(jnp.bfloat16)
        back_sum = block_sum(dy_rows, down_eff.T)
        gate_grad = (back_sum * up_sum * gate_sig * (1.0 + gate_sum * (1.0 - gate_sig))).astype(jnp.bfloat16)
        up_grad = (back_sum * gate_sum * gate_sig).astype(jnp.bfloat16)
        input_grad = jnp.dot(gate_grad, gate_eff.T, preferred_element_type=jnp.float32)
        input_grad = (input_grad + jnp.dot(up_grad, up_eff.T, preferred_element_type=jnp.float32)).astype(jnp.bfloat16)
        gate_term = masked(jnp.dot(x_rows.T, gate_grad, preferred_element_type=jnp.float32), gate_keep)
        up_term = masked(jnp.dot(x_rows.T, up_grad, preferred_element_type=jnp.float32), up_keep)
        down_term = masked(jnp.dot(hidden.T, dy_rows, preferred_element_type=jnp.float32), down_keep)
        gate_total = gate_total + rounded(gate_term)
        up_total = up_total + rounded(up_term)
        down_total = down_total + rounded(down_term)
        mixed_list.append(mixed.reshape(N_COL, TOK_DEV, D))
        input_list.append(input_grad.reshape(N_COL, TOK_DEV, D))
    mixed_all = jnp.stack(mixed_list, axis=1).reshape(TOKENS, D)
    input_all = jnp.stack(input_list, axis=1).reshape(TOKENS, D)
    return (mixed_all, input_all, gate_total.astype(jnp.bfloat16), up_total.astype(jnp.bfloat16), down_total.astype(jnp.bfloat16))
```

```python
import jax
import jax.numpy as jnp
from jax import lax
from jax.experimental import pallas as pl
from jax.experimental.pallas import tpu as pltpu
from jax.sharding import PartitionSpec as P

BF16 = jnp.bfloat16
F32 = jnp.float32
PLAIN = (((1,), (0,)), ((), ()))
FLIPPED = (((1,), (1,)), ((), ()))
OVER_ROWS = (((0,), (0,)), ((), ()))


def dot(left, right, dims):
    return lax.dot_general(left, right, dims, preferred_element_type=F32)


def prune(source, keep, target):
    rows, cols = keep.shape
    height, width = source.shape[0] // rows, source.shape[1] // cols
    for a in range(rows):
        for b in range(cols):
            block = (pl.ds(a * height, height), pl.ds(b * width, width))
            value = source[block]
            target[block] = jnp.where(keep[a, b] != 0, value, jnp.zeros_like(value))


def forward_body(panel, gate, up, down, gate_keep, up_keep, down_keep, part, gate_eff, up_eff, down_eff):
    model = gate.shape[0]
    hidden = gate.shape[1]
    prune(gate, gate_keep, gate_eff)
    prune(up, up_keep, up_eff)
    prune(down, down_keep, down_eff)
    tokens = panel[:, :model]
    grads = panel[:, model:]
    part[:, :hidden] = dot(tokens, gate_eff[...], PLAIN).astype(BF16)
    part[:, hidden : 2 * hidden] = dot(tokens, up_eff[...], PLAIN).astype(BF16)
    part[:, 2 * hidden :] = dot(grads, down_eff[...], FLIPPED).astype(BF16)


def pointwise_body(parts, out):
    width = parts.shape[2] // 3
    total = jnp.sum(parts[...].astype(F32), axis=0)
    gate = total[:, :width]
    up = total[:, width : 2 * width]
    back = total[:, 2 * width :]
    sig = jax.nn.sigmoid(gate)
    hidden = (gate * sig * up).astype(BF16)
    gate_grad = (back * up * sig * (1.0 + gate * (1.0 - sig))).astype(BF16)
    up_grad = (back * gate * sig).astype(BF16)
    for copy in range(out.shape[0]):
        out[copy, :, :width] = hidden
        out[copy, :, width : 2 * width] = gate_grad
        out[copy, :, 2 * width :] = up_grad


def outputs_body(mid, gate_eff, up_eff, down_eff, out):
    width = gate_eff.shape[1]
    model = gate_eff.shape[0]
    out[:, :model] = dot(mid[:, :width], down_eff[...], PLAIN).astype(BF16)
    out[:, model:] = (
        dot(mid[:, width : 2 * width], gate_eff[...], FLIPPED)
        + dot(mid[:, 2 * width :], up_eff[...], FLIPPED)
    ).astype(BF16)


def weights_body(panel, mid, gate_keep, up_keep, down_keep, gate_out, up_out, down_out, wide, tall):
    model = gate_out.shape[0]
    width = gate_out.shape[1]
    tokens = panel[:, :model]
    wide[...] = dot(tokens, mid[:, width : 2 * width], OVER_ROWS).astype(BF16)
    prune(wide, gate_keep, gate_out)
    wide[...] = dot(tokens, mid[:, 2 * width :], OVER_ROWS).astype(BF16)
    prune(wide, up_keep, up_out)
    tall[...] = dot(mid[:, :width], panel[:, model:], OVER_ROWS).astype(BF16)
    prune(tall, down_keep, down_out)


def reduce_body(parts, mixed, input_grad):
    model = mixed.shape[1]
    total = jnp.sum(parts[...].astype(F32), axis=0)
    mixed[...] = total[:, :model].astype(BF16)
    input_grad[...] = total[:, model:].astype(BF16)


VMEM = pl.BlockSpec(memory_space=pltpu.VMEM)
SMEM = pl.BlockSpec(memory_space=pltpu.SMEM)


def shape(*dims):
    return jax.ShapeDtypeStruct(dims, BF16)


def call(body, ins, outs, scratch=()):
    return pl.pallas_call(
        body,
        in_specs=ins,
        out_specs=[VMEM] * len(outs),
        out_shape=list(outs),
        scratch_shapes=list(scratch),
    )


def per_device(tokens, grad_out, gate_weight, up_weight, down_weight, gate_keep, up_keep, down_keep):
    rows = lax.axis_size("row")
    cols = lax.axis_size("col")
    block, model = tokens.shape
    width = gate_weight.shape[1]
    held = cols * block
    joined = jnp.concatenate([tokens, grad_out], axis=1)
    panel = lax.all_to_all(
        jnp.broadcast_to(joined[None], (cols, block, 2 * model)), "col", 0, 0
    ).reshape(held, 2 * model)
    part, gate_eff, up_eff, down_eff = call(
        forward_body,
        [VMEM] * 4 + [SMEM] * 3,
        [shape(held, 3 * width), shape(model, width), shape(model, width), shape(width, model)],
    )(panel, gate_weight, up_weight, down_weight, gate_keep, up_keep, down_keep)
    share = held // rows
    parts = lax.all_to_all(part.reshape(rows, share, 3 * width), "row", 0, 0)
    (spread,) = call(pointwise_body, [VMEM], [shape(rows, share, 3 * width)])(parts)
    mid = lax.all_to_all(spread, "row", 0, 0).reshape(held, 3 * width)
    own = call(
        weights_body,
        [VMEM] * 2 + [SMEM] * 3,
        [shape(model, width), shape(model, width), shape(width, model)],
        [pltpu.VMEM((model, width), BF16), pltpu.VMEM((width, model), BF16)],
    )(panel, mid, gate_keep, up_keep, down_keep)
    swap = [(0, 1), (1, 0)]
    other = [lax.ppermute(term, "rep", swap) for term in own]
    (out,) = call(outputs_body, [VMEM] * 4, [shape(held, 2 * model)])(
        mid, gate_eff, up_eff, down_eff
    )
    pieces = lax.all_to_all(out.reshape(cols, block, 2 * model), "col", 0, 0)
    mixed, input_grad = call(reduce_body, [VMEM], [shape(block, model)] * 2)(pieces)
    totals = [
        (mine.astype(F32) + theirs.astype(F32)).astype(BF16) for mine, theirs in zip(own, other)
    ]
    return (mixed, input_grad, *totals)


def solution(mesh):
    return jax.shard_map(
        per_device,
        mesh=mesh,
        in_specs=(
            P(("col", "rep"), "row"),
            P(("col", "rep"), "row"),
            P("row", "col"),
            P("row", "col"),
            P("col", "row"),
            P("row", "col"),
            P("row", "col"),
            P("col", "row"),
        ),
        out_specs=(
            P(("col", "rep"), "row"),
            P(("col", "rep"), "row"),
            P("row", "col"),
            P("row", "col"),
            P("col", "row"),
        ),
        check_vma=False,
    )
```

```python
import jax
import jax.numpy as jnp
from jax import lax
from jax.experimental import pallas as pl
from jax.experimental.pallas import tpu as pltpu
from jax.sharding import Mesh, PartitionSpec as P


BF16 = jnp.bfloat16
F32 = jnp.float32
PLAIN = (((1,), (0,)), ((), ()))
FLIPPED = (((1,), (1,)), ((), ()))
NEAR = 4
LIMIT = 24 * 1024 * 1024
HALVES = 2
SWAP = [(0, 1), (1, 0)]
VMEM = pl.BlockSpec(memory_space=pltpu.VMEM)
SMEM = pl.BlockSpec(memory_space=pltpu.SMEM)


def dot(left, right, dims):
    return lax.dot_general(left, right, dims, preferred_element_type=F32)


def shape(*dims):
    return jax.ShapeDtypeStruct(dims, BF16)


def call(body, ins, outs, scratch=()):
    return pl.pallas_call(
        body,
        in_specs=ins,
        out_specs=[VMEM] * len(outs),
        out_shape=list(outs),
        scratch_shapes=list(scratch),
        compiler_params=pltpu.CompilerParams(vmem_limit_bytes=LIMIT),
    )


def near(value):
    return pltpu.with_memory_space_constraint(value, pltpu.VMEM)


def local(*dims):
    return pltpu.VMEM(dims, BF16)


def mark_body(rep, out):
    out[0] = rep[0]
    out[1] = rep[1]


def mark(rep):
    return pl.pallas_call(
        mark_body,
        in_specs=[SMEM],
        out_specs=SMEM,
        out_shape=jax.ShapeDtypeStruct((2,), jnp.int32),
    )(rep)


def half_of(index, size):
    return pl.ds(pl.multiple_of(index * size, size), size)


def pick(keep, value):
    return jnp.where(keep != 0, value, jnp.zeros_like(value))


def prepare_body(place_of, gate, up, down, gate_keep, up_keep, down_keep, *refs):
    *outs, full, rows, tall = refs
    out = full
    part, own = place_of[0], place_of[1]
    size = rows.shape[0]
    blocks = gate_keep.shape[1]
    span = rows.shape[1] // blocks
    units = out.shape[1] // 3
    for place, source, keep in ((0, gate, gate_keep), (1, up, up_keep)):
        value = source[half_of(part, size), :]
        for b in range(blocks):
            rows[:, b * span : (b + 1) * span] = pick(keep[part, b], value[:, b * span : (b + 1) * span])
        turned = rows[...].T
        for b in range(out.shape[0]):
            out[b, place * units : (place + 1) * units, :] = turned[b * units : (b + 1) * units]
    value = down[:, half_of(part, size)]
    for b in range(blocks):
        tall[b * span : (b + 1) * span, :] = pick(down_keep[b, part], value[b * span : (b + 1) * span])
    for b in range(out.shape[0]):
        out[b, 2 * units : 3 * units, :] = tall[b * units : (b + 1) * units, :]
    for k, target in enumerate(outs):
        target[...] = full[own ^ k]


def pack_body(place_of, *refs):
    *pieces, out = refs
    own = place_of[1]
    for k, piece in enumerate(pieces):
        out[own ^ k] = piece[...]


def panel_of(panel, b):
    cols, _, block, width = panel.shape
    return panel[:, b].reshape(cols * block, width)


def partial_body(rep, panel, mine, theirs, weights, part):
    own = rep[0]
    size = mine.shape[2]
    weights[:, :, half_of(own, size)] = mine[...]
    weights[:, :, half_of(1 - own, size)] = theirs[...]
    units = weights.shape[1] // 3
    model = weights.shape[2]
    far, _, piece, _ = part.shape
    both = [None] * 2
    for b in range(weights.shape[0]):
        rows = panel_of(panel, b)
        first = dot(weights[b, : 2 * units, :], rows[:, :model], FLIPPED)
        last = dot(weights[b, 2 * units :, :], rows[:, model:], FLIPPED)
        both = [first, last] if b == 0 else [both[0] + first, both[1] + last]
    for a in range(far):
        part[a, 0] = both[0][a * piece : (a + 1) * piece].astype(BF16)
        part[a, 1] = both[0][units + a * piece : units + (a + 1) * piece].astype(BF16)
        part[a, 2] = both[1][a * piece : (a + 1) * piece].astype(BF16)


def pointwise_body(parts, out):
    total = parts[0].astype(F32)
    for a in range(1, parts.shape[0]):
        total = total + parts[a].astype(F32)
    gate, up, back = total[0], total[1], total[2]
    sig = jax.nn.sigmoid(gate)
    out[0] = (gate * sig * up).astype(BF16)
    out[1] = (back * up * sig * (1.0 + gate * (1.0 - sig))).astype(BF16)
    out[2] = (back * gate * sig).astype(BF16)


def assemble(mid, place):
    return jnp.concatenate([mid[a, place].astype(F32) for a in range(mid.shape[0])], axis=0)


def outputs_body(mid, weights, out):
    units = weights.shape[1] // 3
    model = weights.shape[2]
    cols, near, block, _ = out.shape
    hidden, gate, up = (assemble(mid, m).T.astype(BF16) for m in range(3))
    for b in range(near):
        ahead = dot(hidden, weights[b, 2 * units :, :], PLAIN)
        behind = dot(gate, weights[b, :units, :], PLAIN) + dot(up, weights[b, units : 2 * units, :], PLAIN)
        out[:, b, :, :model] = ahead.astype(BF16).reshape(cols, block, model)
        out[:, b, :, model:] = behind.astype(BF16).reshape(cols, block, model)


def terms_body(rep, panel, mid, keep, give, full):
    own = rep[0]
    size = keep.shape[2]
    near, stacked, model = full.shape
    units = stacked // 3
    hidden, gate, up = (assemble(mid, m).astype(BF16) for m in range(3))
    for b in range(near):
        rows = panel_of(panel, b)
        full[b, :units, :] = dot(gate, rows[:, :model], PLAIN).astype(BF16)
        full[b, units : 2 * units, :] = dot(up, rows[:, :model], PLAIN).astype(BF16)
        full[b, 2 * units :, :] = dot(hidden, rows[:, model:], PLAIN).astype(BF16)
    keep[...] = full[:, :, half_of(own, size)]
    give[...] = full[:, :, half_of(1 - own, size)]


def add_body(place_of, left, right, *outs):
    own = place_of[1]
    for k, out in enumerate(outs):
        member = own ^ k
        out[...] = (left[member].astype(F32) + right[member].astype(F32)).astype(BF16)


def fold_body(pieces, out):
    total = pieces[0].astype(F32)
    for c in range(1, pieces.shape[0]):
        total = total + pieces[c].astype(F32)
    out[...] = total.astype(BF16)


def finish_body(pieces, mixed, input_grad):
    model = mixed.shape[1]
    total = pieces[0].astype(F32)
    for b in range(1, pieces.shape[0]):
        total = total + pieces[b].astype(F32)
    mixed[...] = total[:, :model].astype(BF16)
    input_grad[...] = total[:, model:].astype(BF16)


def unpack_body(rep, mine, theirs, gate_keep, up_keep, down_keep, gate_out, up_out, down_out, tall):
    own = rep[0]
    near, stacked, size = mine.shape
    units = stacked // 3
    blocks = gate_keep.shape[1]
    span = gate_out.shape[1] // blocks
    for source, part in ((mine, own), (theirs, 1 - own)):
        for place, keep, out in ((0, gate_keep, gate_out), (1, up_keep, up_out), (2, down_keep, down_out)):
            for b in range(near):
                tall[b * units : (b + 1) * units, :] = source[b, place * units : (place + 1) * units, :]
            if place < 2:
                turned = tall[...].T
                for b in range(blocks):
                    out[half_of(part, size), b * span : (b + 1) * span] = pick(
                        keep[part, b], turned[:, b * span : (b + 1) * span]
                    )
            else:
                for b in range(blocks):
                    out[b * span : (b + 1) * span, half_of(part, size)] = pick(
                        keep[b, part], tall[b * span : (b + 1) * span, :]
                    )


def spread(value, axis):
    count = lax.axis_size(axis)
    return lax.all_to_all(jnp.broadcast_to(value[None], (count,) + value.shape), axis, 0, 0)


def exchange(pieces, count):
    own, *others = pieces
    moved = [
        lax.ppermute(piece, "b", [(i, i ^ k) for i in range(count)])
        for k, piece in enumerate(others, 1)
    ]
    return [own, *moved]


def per_device(tokens, grad_out, gate_weight, up_weight, down_weight, gate_keep, up_keep, down_keep):
    far = lax.axis_size("a")
    group = lax.axis_size("b")
    cols = lax.axis_size("col")
    block, model = tokens.shape
    width = gate_weight.shape[1]
    units = width // group
    piece = units // far
    held = cols * block
    size = model // HALVES
    place = jnp.stack([lax.axis_index("rep"), lax.axis_index("b")]).astype(jnp.int32)
    joined = jnp.concatenate([tokens, grad_out], axis=1)
    panel = spread(joined, "b")
    sent = call(
        prepare_body,
        [SMEM] + [VMEM] * 3 + [SMEM] * 3,
        [local(3 * units, size)] * group,
        [pltpu.VMEM((group, 3 * units, size), BF16), pltpu.VMEM((size, width), BF16), pltpu.VMEM((width, size), BF16)],
    )(place, gate_weight, up_weight, down_weight, gate_keep, up_keep, down_keep)
    got = exchange(sent, group)
    panel = spread(panel, "col")
    (mine,) = call(pack_body, [SMEM] + [VMEM] * group, [local(group, 3 * units, size)])(
        place, *map(near, got)
    )
    theirs = lax.ppermute(mine, "rep", SWAP)
    first_mark = mark(place)
    weights, part = call(
        partial_body,
        [SMEM] + [VMEM] * 3,
        [local(group, 3 * units, model), local(far, 3, piece, held)],
    )(first_mark, near(panel), near(mine), near(theirs))
    parts = lax.all_to_all(part, "a", 0, 0)
    (own,) = call(pointwise_body, [VMEM], [local(3, piece, held)])(near(parts))
    mid = lax.all_gather(own.reshape(3 * piece, held), "a", axis=0, tiled=True)
    mid = near(mid.reshape(far, 3, piece, held))
    keep, give = call(
        terms_body,
        [SMEM] + [VMEM] * 2,
        [local(group, 3 * units, size)] * 2,
        [pltpu.VMEM((group, 3 * units, model), BF16)],
    )(place, near(panel), mid)
    taken = lax.ppermute(give, "rep", SWAP)
    (out,) = call(outputs_body, [VMEM] * 2, [local(cols, group, block, 2 * model)])(
        mid, weights
    )
    pieces = lax.all_to_all(out, "col", 0, 0)
    terms = call(add_body, [SMEM] + [VMEM] * 2, [local(3 * units, size)] * group)(
        place, keep, near(taken)
    )
    terms = exchange(terms, group)
    second_mark = mark(first_mark)
    (folded,) = call(fold_body, [VMEM], [local(group, block, 2 * model)])(near(pieces))
    last = lax.all_to_all(folded, "b", 0, 0)
    (terms,) = call(pack_body, [SMEM] + [VMEM] * group, [local(group, 3 * units, size)])(second_mark, *map(near, terms))
    others = lax.ppermute(terms, "rep", SWAP)
    mixed, input_grad = call(finish_body, [VMEM], [shape(block, model)] * 2)(near(last))
    gate_grad, up_grad, down_grad = call(
        unpack_body,
        [SMEM] + [VMEM] * 2 + [SMEM] * 3,
        [shape(model, width), shape(model, width), shape(width, model)],
        [pltpu.VMEM((width, size), BF16)],
    )(place, near(terms), near(others), gate_keep, up_keep, down_keep)
    return (mixed, input_grad, gate_grad, up_grad, down_grad)


def solution(mesh):
    rows = mesh.shape["row"]
    grid = Mesh(
        mesh.devices.reshape(rows // NEAR, NEAR, mesh.shape["col"], mesh.shape["rep"]),
        ("a", "b", "col", "rep"),
    )
    row = ("a", "b")
    return jax.shard_map(
        per_device,
        mesh=grid,
        in_specs=(
            P(("col", "rep"), row),
            P(("col", "rep"), row),
            P(row, "col"),
            P(row, "col"),
            P("col", row),
            P(row, "col"),
            P(row, "col"),
            P("col", row),
        ),
        out_specs=(
            P(("col", "rep"), row),
            P(("col", "rep"), row),
            P(row, "col"),
            P(row, "col"),
            P("col", row),
        ),
        check_vma=False,
    )
```

```python
import jax
import jax.numpy as jnp
from jax import lax
from jax.experimental import pallas as pl
from jax.experimental.pallas import tpu as pltpu
from jax.sharding import Mesh, PartitionSpec as P


BF16 = jnp.bfloat16
F32 = jnp.float32
PLAIN = (((1,), (0,)), ((), ()))
FLIPPED = (((1,), (1,)), ((), ()))
NEAR = 4
LIMIT = 24 * 1024 * 1024
HALVES = 2
SWAP = [(0, 1), (1, 0)]
VMEM = pl.BlockSpec(memory_space=pltpu.VMEM)
SMEM = pl.BlockSpec(memory_space=pltpu.SMEM)


def dot(left, right, dims):
    return lax.dot_general(left, right, dims, preferred_element_type=F32)


def shape(*dims):
    return jax.ShapeDtypeStruct(dims, BF16)


def call(body, ins, outs, scratch=()):
    return pl.pallas_call(
        body,
        in_specs=ins,
        out_specs=[VMEM] * len(outs),
        out_shape=list(outs),
        scratch_shapes=list(scratch),
        compiler_params=pltpu.CompilerParams(vmem_limit_bytes=LIMIT),
    )


def near(value):
    return pltpu.with_memory_space_constraint(value, pltpu.VMEM)


def local(*dims):
    return pltpu.VMEM(dims, BF16)


def mark_body(out):
    out[...] = jnp.zeros_like(out)


def next_mark_body(before, out):
    out[...] = before[...]


def distant(value):
    return pltpu.with_memory_space_constraint(value, pltpu.HBM)


def half_of(index, size):
    return pl.ds(pl.multiple_of(index * size, size), size)


def pick(keep, value):
    return jnp.where(keep != 0, value, jnp.zeros_like(value))


def prepare_body(gate, up, down, gate_keep, up_keep, down_keep, *refs):
    *outs, full, rows, tall = refs
    out = full
    part, own = lax.axis_index("rep"), lax.axis_index("b")
    size = rows.shape[0]
    blocks = gate_keep.shape[1]
    span = rows.shape[1] // blocks
    units = out.shape[1] // 3
    for place, source, keep in ((0, gate, gate_keep), (1, up, up_keep)):
        value = source[half_of(part, size), :]
        for b in range(blocks):
            rows[:, b * span : (b + 1) * span] = pick(keep[part, b], value[:, b * span : (b + 1) * span])
        turned = rows[...].T
        for b in range(out.shape[0]):
            out[b, place * units : (place + 1) * units, :] = turned[b * units : (b + 1) * units]
    value = down[:, half_of(part, size)]
    for b in range(blocks):
        tall[b * span : (b + 1) * span, :] = pick(down_keep[part, b], value[b * span : (b + 1) * span])
    for b in range(out.shape[0]):
        out[b, 2 * units : 3 * units, :] = tall[b * units : (b + 1) * units, :]
    for k, target in enumerate(outs):
        target[...] = full[own ^ k]


def pack_body(*refs):
    *pieces, out = refs
    own = lax.axis_index("b")
    for k, piece in enumerate(pieces):
        out[own ^ k] = piece[...]


def panel_of(panel, b):
    cols, _, block, width = panel.shape
    return panel[:, b].reshape(cols * block, width)


def partial_body(marked, panel, mine, theirs, weights, part):
    own = lax.axis_index("rep")
    size = mine.shape[2]
    weights[:, :, half_of(own, size)] = mine[...]
    weights[:, :, half_of(1 - own, size)] = theirs[...]
    units = weights.shape[1] // 3
    model = weights.shape[2]
    far, _, piece, _ = part.shape
    both = [None] * 2
    for b in range(weights.shape[0]):
        rows = panel_of(panel, b)
        first = dot(weights[b, : 2 * units, :], rows[:, :model], FLIPPED)
        last = dot(weights[b, 2 * units :, :], rows[:, model:], FLIPPED)
        both = [first, last] if b == 0 else [both[0] + first, both[1] + last]
    for a in range(far):
        part[a, 0] = both[0][a * piece : (a + 1) * piece].astype(BF16)
        part[a, 1] = both[0][units + a * piece : units + (a + 1) * piece].astype(BF16)
        part[a, 2] = both[1][a * piece : (a + 1) * piece].astype(BF16)


def pointwise_body(parts, out):
    total = parts[0].astype(F32)
    for a in range(1, parts.shape[0]):
        total = total + parts[a].astype(F32)
    gate, up, back = total[0], total[1], total[2]
    sig = jax.nn.sigmoid(gate)
    out[0] = (gate * sig * up).astype(BF16)
    out[1] = (back * up * sig * (1.0 + gate * (1.0 - sig))).astype(BF16)
    out[2] = (back * gate * sig).astype(BF16)


def assemble(mid, place):
    return jnp.concatenate([mid[a, place].astype(F32) for a in range(mid.shape[0])], axis=0)


def outputs_body(mid, weights, out):
    units = weights.shape[1] // 3
    model = weights.shape[2]
    cols, near, block, _ = out.shape
    hidden, gate, up = (assemble(mid, m).T.astype(BF16) for m in range(3))
    for b in range(near):
        ahead = dot(hidden, weights[b, 2 * units :, :], PLAIN)
        behind = dot(gate, weights[b, :units, :], PLAIN) + dot(up, weights[b, units : 2 * units, :], PLAIN)
        out[:, b, :, :model] = ahead.astype(BF16).reshape(cols, block, model)
        out[:, b, :, model:] = behind.astype(BF16).reshape(cols, block, model)


def terms_body(panel, mid, keep, give, full):
    own = lax.axis_index("rep")
    size = keep.shape[2]
    near, stacked, model = full.shape
    units = stacked // 3
    hidden, gate, up = (assemble(mid, m).astype(BF16) for m in range(3))
    for b in range(near):
        rows = panel_of(panel, b)
        full[b, :units, :] = dot(gate, rows[:, :model], PLAIN).astype(BF16)
        full[b, units : 2 * units, :] = dot(up, rows[:, :model], PLAIN).astype(BF16)
        full[b, 2 * units :, :] = dot(hidden, rows[:, model:], PLAIN).astype(BF16)
    keep[...] = full[:, :, half_of(own, size)]
    give[...] = full[:, :, half_of(1 - own, size)]


def add_body(left, right, *outs):
    own = lax.axis_index("b")
    for k, out in enumerate(outs):
        member = own ^ k
        out[...] = (left[member].astype(F32) + right[member].astype(F32)).astype(BF16)


def fold_body(pieces, out):
    total = pieces[0].astype(F32)
    for c in range(1, pieces.shape[0]):
        total = total + pieces[c].astype(F32)
    out[...] = total.astype(BF16)


def finish_body(pieces, mixed, input_grad):
    model = mixed.shape[1]
    total = pieces[0].astype(F32)
    for b in range(1, pieces.shape[0]):
        total = total + pieces[b].astype(F32)
    mixed[...] = total[:, :model].astype(BF16)
    input_grad[...] = total[:, model:].astype(BF16)


def unpack_body(marked, mine, theirs, gate_keep, up_keep, down_keep, gate_out, up_out, down_out, tall):
    own = lax.axis_index("rep")
    near, stacked, size = mine.shape
    units = stacked // 3
    blocks = gate_keep.shape[1]
    span = gate_out.shape[1] // blocks
    for source, part in ((mine, own), (theirs, 1 - own)):
        for place, keep, out in ((0, gate_keep, gate_out), (1, up_keep, up_out), (2, down_keep, down_out)):
            for b in range(near):
                tall[b * units : (b + 1) * units, :] = source[b, place * units : (place + 1) * units, :]
            if place < 2:
                turned = tall[...].T
                for b in range(blocks):
                    out[half_of(part, size), b * span : (b + 1) * span] = pick(
                        keep[part, b], turned[:, b * span : (b + 1) * span]
                    )
            else:
                for b in range(blocks):
                    out[b * span : (b + 1) * span, half_of(part, size)] = pick(
                        keep[part, b], tall[b * span : (b + 1) * span, :]
                    )


def spread(value, axis):
    count = lax.axis_size(axis)
    return lax.all_to_all(jnp.broadcast_to(value[None], (count,) + value.shape), axis, 0, 0)


def exchange(pieces, count):
    own, *others = pieces
    moved = [
        lax.ppermute(piece, "b", [(i, i ^ k) for i in range(count)])
        for k, piece in enumerate(others, 1)
    ]
    return [own, *moved]


def per_device(tokens, grad_out, gate_weight, up_weight, down_weight, gate_keep, up_keep, down_keep):
    far = lax.axis_size("a")
    group = lax.axis_size("b")
    cols = lax.axis_size("col")
    block, model = tokens.shape
    width = gate_weight.shape[1]
    units = width // group
    piece = units // far
    held = cols * block
    size = model // HALVES
    joined = jnp.concatenate([tokens, grad_out], axis=1)
    down_keep = down_keep.T
    panel = spread(joined, "b")
    sent = call(
        prepare_body,
        [VMEM] * 3 + [SMEM] * 3,
        [local(3 * units, size)] * group,
        [pltpu.VMEM((group, 3 * units, size), BF16), pltpu.VMEM((size, width), BF16), pltpu.VMEM((width, size), BF16)],
    )(*map(distant, (gate_weight, up_weight, down_weight, gate_keep, up_keep, down_keep)))
    got = exchange(sent, group)
    panel = spread(panel, "col")
    (mine,) = call(pack_body, [VMEM] * group, [local(group, 3 * units, size)])(
        *map(near, got)
    )
    theirs = lax.ppermute(mine, "rep", SWAP)
    (first_mark,) = call(mark_body, [], [local(16, 128)])()
    weights, part = call(
        partial_body,
        [VMEM] * 4,
        [local(group, 3 * units, model), local(far, 3, piece, held)],
    )(first_mark, near(panel), near(mine), near(theirs))
    parts = lax.all_to_all(part, "a", 0, 0)
    (own,) = call(pointwise_body, [VMEM], [local(3, piece, held)])(near(parts))
    mid = lax.all_gather(own.reshape(3 * piece, held), "a", axis=0, tiled=True)
    mid = near(mid.reshape(far, 3, piece, held))
    (out,) = call(outputs_body, [VMEM] * 2, [local(cols, group, block, 2 * model)])(
        mid, weights
    )
    pieces = lax.all_to_all(out, "col", 0, 0)
    keep, give = call(
        terms_body,
        [VMEM] * 2,
        [local(group, 3 * units, size)] * 2,
        [pltpu.VMEM((group, 3 * units, model), BF16)],
    )(near(panel), mid)
    taken = lax.ppermute(give, "rep", SWAP)
    terms = call(add_body, [VMEM] * 2, [local(3 * units, size)] * group)(
        keep, near(taken)
    )
    terms = exchange(terms, group)
    (second_mark,) = call(next_mark_body, [VMEM], [local(16, 128)])(first_mark)
    (folded,) = call(fold_body, [VMEM], [local(group, block, 2 * model)])(near(pieces))
    last = lax.all_to_all(folded, "b", 0, 0)
    (terms,) = call(pack_body, [VMEM] * group, [local(group, 3 * units, size)])(
        *map(near, terms)
    )
    others = lax.ppermute(terms, "rep", SWAP)
    mixed, input_grad = call(finish_body, [VMEM], [shape(block, model)] * 2)(near(last))
    gate_grad, up_grad, down_grad = call(
        unpack_body,
        [VMEM] * 3 + [SMEM] * 3,
        [shape(model, width), shape(model, width), shape(width, model)],
        [pltpu.VMEM((width, size), BF16)],
    )(second_mark, near(terms), near(others), *map(distant, (gate_keep, up_keep, down_keep)))
    return (mixed, input_grad, gate_grad, up_grad, down_grad)


def solution(mesh):
    rows = mesh.shape["row"]
    grid = Mesh(
        mesh.devices.reshape(rows // NEAR, NEAR, mesh.shape["col"], mesh.shape["rep"]),
        ("a", "b", "col", "rep"),
    )
    row = ("a", "b")
    return jax.shard_map(
        per_device,
        mesh=grid,
        in_specs=(
            P(("col", "rep"), row),
            P(("col", "rep"), row),
            P(row, "col"),
            P(row, "col"),
            P("col", row),
            P(row, "col"),
            P(row, "col"),
            P("col", row),
        ),
        out_specs=(
            P(("col", "rep"), row),
            P(("col", "rep"), row),
            P(row, "col"),
            P(row, "col"),
            P("col", row),
        ),
        check_vma=False,
    )
```

```python
import jax
import jax.numpy as jnp
from jax import lax
from jax.experimental import pallas as pl
from jax.experimental.pallas import tpu as pltpu
from jax.sharding import Mesh, PartitionSpec as P


BF16 = jnp.bfloat16
F32 = jnp.float32
PLAIN = (((1,), (0,)), ((), ()))
FLIPPED = (((1,), (1,)), ((), ()))
NEAR = 4
LIMIT = 16 * 1024 * 1024
HALVES = 2
SWAP = [(0, 1), (1, 0)]
VMEM = pl.BlockSpec(memory_space=pltpu.VMEM)
SMEM = pl.BlockSpec(memory_space=pltpu.SMEM)


def dot(left, right, dims):
    return lax.dot_general(left, right, dims, preferred_element_type=F32)


def shape(*dims):
    return jax.ShapeDtypeStruct(dims, BF16)


def call(body, ins, outs, scratch=()):
    return pl.pallas_call(
        body,
        in_specs=ins,
        out_specs=[VMEM] * len(outs),
        out_shape=list(outs),
        scratch_shapes=list(scratch),
        compiler_params=pltpu.CompilerParams(vmem_limit_bytes=LIMIT),
    )


def near(value):
    return pltpu.with_memory_space_constraint(value, pltpu.VMEM)


def local(*dims):
    return pltpu.VMEM(dims, BF16)


def outside(*dims):
    return pltpu.HBM(dims, BF16)


def mark_body(out):
    out[...] = jnp.zeros_like(out)


def next_mark_body(before, out):
    out[...] = before[...]


def distant(value):
    return pltpu.with_memory_space_constraint(value, pltpu.HBM)


def half_of(index, size):
    return pl.ds(pl.multiple_of(index * size, size), size)


def pick(keep, value):
    return jnp.where(keep != 0, value, jnp.zeros_like(value))


def members(own):
    rep = lax.axis_index("rep")
    return own ^ (1 + rep), own ^ (2 - rep), own ^ 3


def prepare_body(gate, up, down, gate_keep, up_keep, down_keep, stay, whole, part, full, rows, tall):
    own, rep = lax.axis_index("b"), lax.axis_index("rep")
    blocks = gate_keep.shape[1]
    span = gate.shape[1] // blocks
    size = part.shape[1]
    units = stay.shape[0] // 3
    for place, source, keep in ((0, gate, gate_keep), (1, up, up_keep)):
        for h in range(HALVES):
            for b in range(blocks):
                cut = (slice(h * size, (h + 1) * size), slice(b * span, (b + 1) * span))
                rows[cut] = pick(keep[h, b], source[cut])
        turned = rows[...].T
        for b in range(full.shape[0]):
            full[b, place * units : (place + 1) * units, :] = turned[b * units : (b + 1) * units]
    for h in range(HALVES):
        for b in range(blocks):
            cut = (slice(b * span, (b + 1) * span), slice(h * size, (h + 1) * size))
            tall[cut] = pick(down_keep[h, b], down[cut])
    for b in range(full.shape[0]):
        full[b, 2 * units : 3 * units, :] = tall[b * units : (b + 1) * units, :]
    first, _, last = members(own)
    stay[...] = full[own]
    whole[...] = full[first]
    part[...] = full[last, :, half_of(rep, size)]


def pack_body(whole, part, out):
    width = whole.shape[1]
    out[:, :width] = whole[...]
    out[:, width:] = part[...]


def panel_of(panel, b):
    cols, _, block, width = panel.shape
    return panel[:, b].reshape(cols * block, width)


def partial_body(marked, panel, stay, whole, part_in, theirs, weights, part):
    own, rep = lax.axis_index("b"), lax.axis_index("rep")
    size = part_in.shape[1]
    width = weights.shape[2]
    first, second, last = members(own)
    weights[own] = stay[...]
    weights[first] = whole[...]
    weights[second] = theirs[:, :width]
    weights[last, :, half_of(rep, size)] = part_in[...]
    weights[last, :, half_of(1 - rep, size)] = theirs[:, width:]
    units = weights.shape[1] // 3
    model = weights.shape[2]
    far, _, piece, _ = part.shape
    both = [None] * 2
    for b in range(weights.shape[0]):
        rows = panel_of(panel, b)
        first = dot(weights[b, : 2 * units, :], rows[:, :model], FLIPPED)
        last = dot(weights[b, 2 * units :, :], rows[:, model:], FLIPPED)
        both = [first, last] if b == 0 else [both[0] + first, both[1] + last]
    for a in range(far):
        part[a, 0] = both[0][a * piece : (a + 1) * piece].astype(BF16)
        part[a, 1] = both[0][units + a * piece : units + (a + 1) * piece].astype(BF16)
        part[a, 2] = both[1][a * piece : (a + 1) * piece].astype(BF16)


def pointwise_body(parts, out):
    total = parts[0].astype(F32)
    for a in range(1, parts.shape[0]):
        total = total + parts[a].astype(F32)
    gate, up, back = total[0], total[1], total[2]
    sig = jax.nn.sigmoid(gate)
    out[0] = (gate * sig * up).astype(BF16)
    out[1] = (back * up * sig * (1.0 + gate * (1.0 - sig))).astype(BF16)
    out[2] = (back * gate * sig).astype(BF16)


def assemble(mid, place):
    return jnp.concatenate([mid[a, place].astype(F32) for a in range(mid.shape[0])], axis=0)


def outputs_body(mid, weights, out):
    units = weights.shape[1] // 3
    model = weights.shape[2]
    cols, near, block, _ = out.shape
    hidden, gate, up = (assemble(mid, m).T.astype(BF16) for m in range(3))
    for b in range(near):
        ahead = dot(hidden, weights[b, 2 * units :, :], PLAIN)
        behind = dot(gate, weights[b, :units, :], PLAIN) + dot(up, weights[b, units : 2 * units, :], PLAIN)
        out[:, b, :, :model] = ahead.astype(BF16).reshape(cols, block, model)
        out[:, b, :, model:] = behind.astype(BF16).reshape(cols, block, model)


def terms_body(marked, panel, other_panel, mid, other_mid, stay, whole, part, full):
    own, rep = lax.axis_index("b"), lax.axis_index("rep")
    first, _, last = members(own)
    cols, _, block, double = panel.shape
    model = double // 2
    size = part.shape[1]
    units = stay.shape[0] // 3
    sources = [
        (rows, *(assemble(values, m).astype(BF16) for m in range(3)))
        for rows, values in ((panel, mid), (other_panel, other_mid))
    ]

    for member, out in ((own, stay), (first, whole), (last, full)):
        total = [0.0, 0.0, 0.0]
        for rows, hidden, gate, up in sources:
            block_rows = rows[:, member].reshape(cols * block, double)
            total[0] = total[0] + dot(gate, block_rows[:, :model], PLAIN)
            total[1] = total[1] + dot(up, block_rows[:, :model], PLAIN)
            total[2] = total[2] + dot(hidden, block_rows[:, model:], PLAIN)
        for place in range(3):
            out[place * units : (place + 1) * units, :] = total[place].astype(BF16)
    part[...] = full[:, half_of(rep, size)]


def fold_body(pieces, out):
    total = pieces[0].astype(F32)
    for c in range(1, pieces.shape[0]):
        total = total + pieces[c].astype(F32)
    out[...] = total.astype(BF16)


def finish_body(pieces, mixed, input_grad):
    model = mixed.shape[1]
    total = pieces[0].astype(F32)
    for b in range(1, pieces.shape[0]):
        total = total + pieces[b].astype(F32)
    mixed[...] = total[:, :model].astype(BF16)
    input_grad[...] = total[:, model:].astype(BF16)


def unpack_body(
    marked,
    stay,
    whole,
    part,
    theirs,
    gate_keep,
    up_keep,
    down_keep,
    gate_out,
    up_out,
    down_out,
    pieces,
    tall,
):
    own, rep = lax.axis_index("b"), lax.axis_index("rep")
    first, second, last = members(own)
    size = part.shape[1]
    model = stay.shape[1]
    units = stay.shape[0] // 3
    blocks = gate_keep.shape[1]
    span = gate_out.shape[1] // blocks

    pieces[own] = stay[...]
    pieces[first] = whole[...]
    pieces[second] = theirs[:, :model]
    pieces[last, :, half_of(rep, size)] = part[...]
    pieces[last, :, half_of(1 - rep, size)] = theirs[:, model:]
    for place, keep, out in ((0, gate_keep, gate_out), (1, up_keep, up_out), (2, down_keep, down_out)):
        for member in range(pieces.shape[0]):
            tall[member * units : (member + 1) * units, :] = pieces[
                member, place * units : (place + 1) * units, :
            ]
        turned = tall[...].T if place < 2 else None
        for h in range(HALVES):
            for b in range(blocks):
                if place < 2:
                    at = (slice(h * size, (h + 1) * size), slice(b * span, (b + 1) * span))
                    out[at] = pick(keep[h, b], turned[at])
                else:
                    at = (slice(b * span, (b + 1) * span), slice(h * size, (h + 1) * size))
                    out[at] = pick(keep[h, b], tall[at])


def spread(value, axis):
    count = lax.axis_size(axis)
    return lax.all_to_all(jnp.broadcast_to(value[None], (count,) + value.shape), axis, 0, 0)


def exchange(whole, part, group):
    whole_moves = [
        (HALVES * b + r, HALVES * (b ^ (1 + r)) + r) for b in range(group) for r in range(HALVES)
    ]
    return (
        lax.ppermute(whole, ("b", "rep"), whole_moves),
        lax.ppermute(part, "b", [(b, b ^ 3) for b in range(group)]),
    )


def per_device(tokens, grad_out, gate_weight, up_weight, down_weight, gate_keep, up_keep, down_keep):
    far = lax.axis_size("a")
    group = lax.axis_size("b")
    cols = lax.axis_size("col")
    block, model = tokens.shape
    width = gate_weight.shape[1]
    units = width // group
    piece = units // far
    held = cols * block
    size = model // HALVES
    joined = jnp.concatenate([tokens, grad_out], axis=1)
    down_keep = down_keep.T
    panel = spread(joined, "b")
    stay, whole, part = call(
        prepare_body,
        [VMEM] * 3 + [SMEM] * 3,
        [local(3 * units, model)] * 2 + [local(3 * units, size)],
        [
            pltpu.VMEM((group, 3 * units, model), BF16),
            pltpu.VMEM((model, width), BF16),
            pltpu.VMEM((width, model), BF16),
        ],
    )(*map(distant, (gate_weight, up_weight, down_weight, gate_keep, up_keep, down_keep)))
    whole, part = exchange(whole, part, group)
    panel = near(spread(panel, "col"))
    (packed,) = call(pack_body, [VMEM] * 2, [local(3 * units, model + size)])(
        near(whole), near(part)
    )
    theirs = lax.ppermute(packed, "rep", SWAP)
    (first_mark,) = call(mark_body, [], [local(16, 128)])()
    weights, partial = call(
        partial_body,
        [VMEM] * 6,
        [outside(group, 3 * units, model), local(far, 3, piece, held)],
    )(first_mark, panel, stay, near(whole), near(part), near(theirs))
    parts = lax.all_to_all(partial, "a", 0, 0)
    other_panel = lax.ppermute(panel, "rep", SWAP)
    (second_mark,) = call(next_mark_body, [VMEM], [local(16, 128)])(first_mark)
    (own,) = call(pointwise_body, [VMEM], [local(3, piece, held)])(near(parts))
    mid = lax.all_gather(own.reshape(3 * piece, held), "a", axis=0, tiled=True)
    mid = near(mid.reshape(far, 3, piece, held))
    (out,) = call(outputs_body, [VMEM] * 2, [local(cols, group, block, 2 * model)])(
        mid, distant(weights)
    )
    pieces = lax.all_to_all(out, "col", 0, 0)
    other_mid = lax.ppermute(mid, "rep", SWAP)
    stay, whole, part = call(
        terms_body,
        [VMEM] * 5,
        [outside(3 * units, model), local(3 * units, model), local(3 * units, size)],
        [pltpu.VMEM((3 * units, model), BF16)],
    )(second_mark, panel, near(other_panel), mid, near(other_mid))
    whole, part = exchange(whole, part, group)
    (third_mark,) = call(next_mark_body, [VMEM], [local(16, 128)])(second_mark)
    (folded,) = call(fold_body, [VMEM], [local(group, block, 2 * model)])(near(pieces))
    last = lax.all_to_all(folded, "b", 0, 0)
    (packed,) = call(pack_body, [VMEM] * 2, [local(3 * units, model + size)])(
        near(whole), near(part)
    )
    theirs = lax.ppermute(packed, "rep", SWAP)
    mixed, input_grad = call(finish_body, [VMEM], [shape(block, model)] * 2)(near(last))
    gate_grad, up_grad, down_grad = call(
        unpack_body,
        [VMEM] * 5 + [SMEM] * 3,
        [shape(model, width), shape(model, width), shape(width, model)],
        [pltpu.VMEM((group, 3 * units, model), BF16), pltpu.VMEM((width, model), BF16)],
    )(
        third_mark,
        distant(stay),
        near(whole),
        near(part),
        near(theirs),
        *map(distant, (gate_keep, up_keep, down_keep)),
    )
    return (mixed, input_grad, gate_grad, up_grad, down_grad)


def solution(mesh):
    rows = mesh.shape["row"]
    grid = Mesh(
        mesh.devices.reshape(rows // NEAR, NEAR, mesh.shape["col"], mesh.shape["rep"]),
        ("a", "b", "col", "rep"),
    )
    row = ("a", "b")
    return jax.shard_map(
        per_device,
        mesh=grid,
        in_specs=(
            P(("col", "rep"), row),
            P(("col", "rep"), row),
            P(row, "col"),
            P(row, "col"),
            P("col", row),
            P(row, "col"),
            P(row, "col"),
            P("col", row),
        ),
        out_specs=(
            P(("col", "rep"), row),
            P(("col", "rep"), row),
            P(row, "col"),
            P(row, "col"),
            P("col", row),
        ),
        check_vma=False,
    )
```

```python
import jax
import jax.numpy as jnp
from jax import lax
from jax.experimental import pallas as pl
from jax.experimental.pallas import tpu as pltpu
from jax.sharding import Mesh, PartitionSpec as P


BF16 = jnp.bfloat16
F32 = jnp.float32
PLAIN = (((1,), (0,)), ((), ()))
FLIPPED = (((1,), (1,)), ((), ()))
NEAR = 4
LIMIT = 16 * 1024 * 1024
HALVES = 2
SWAP = [(0, 1), (1, 0)]
VMEM = pl.BlockSpec(memory_space=pltpu.VMEM)
SMEM = pl.BlockSpec(memory_space=pltpu.SMEM)


def dot(left, right, dims):
    return lax.dot_general(left, right, dims, preferred_element_type=F32)


def shape(*dims):
    return jax.ShapeDtypeStruct(dims, BF16)


def call(body, ins, outs, scratch=()):
    return pl.pallas_call(
        body,
        in_specs=ins,
        out_specs=[VMEM] * len(outs),
        out_shape=list(outs),
        scratch_shapes=list(scratch),
        compiler_params=pltpu.CompilerParams(vmem_limit_bytes=LIMIT),
    )


def near(value):
    return pltpu.with_memory_space_constraint(value, pltpu.VMEM)


def local(*dims):
    return pltpu.VMEM(dims, BF16)


def outside(*dims):
    return pltpu.HBM(dims, BF16)


def mark_body(out):
    out[...] = jnp.zeros_like(out)


def next_mark_body(before, out):
    out[...] = before[...]


def distant(value):
    return pltpu.with_memory_space_constraint(value, pltpu.HBM)


def half_of(index, size):
    return pl.ds(pl.multiple_of(index * size, size), size)


def pick(keep, value):
    return jnp.where(keep != 0, value, jnp.zeros_like(value))


def members(own):
    rep = lax.axis_index("rep")
    return own ^ (1 + rep), own ^ (2 - rep), own ^ 3


def prepare_body(gate, up, down, gate_keep, up_keep, down_keep, stay, whole, part, full, rows, tall):
    own, rep = lax.axis_index("b"), lax.axis_index("rep")
    blocks = gate_keep.shape[1]
    span = gate.shape[1] // blocks
    size = part.shape[1]
    units = stay.shape[0] // 3
    for place, source, keep in ((0, gate, gate_keep), (1, up, up_keep)):
        for h in range(HALVES):
            for b in range(blocks):
                cut = (slice(h * size, (h + 1) * size), slice(b * span, (b + 1) * span))
                rows[cut] = pick(keep[h, b], source[cut])
        turned = rows[...].T
        for b in range(full.shape[0]):
            full[b, place * units : (place + 1) * units, :] = turned[b * units : (b + 1) * units]
    for h in range(HALVES):
        for b in range(blocks):
            cut = (slice(b * span, (b + 1) * span), slice(h * size, (h + 1) * size))
            tall[cut] = pick(down_keep[h, b], down[cut])
    for b in range(full.shape[0]):
        full[b, 2 * units : 3 * units, :] = tall[b * units : (b + 1) * units, :]
    first, _, last = members(own)
    stay[...] = full[own]
    whole[...] = full[first]
    part[...] = full[last, :, half_of(rep, size)]


def pack_body(whole, part, out):
    width = whole.shape[1]
    out[:, :width] = whole[...]
    out[:, width:] = part[...]


def panel_of(panel, b):
    cols, _, block, width = panel.shape
    return panel[:, b].reshape(cols * block, width)


def partial_body(marked, panel, stay, whole, part_in, theirs, weights, part):
    own, rep = lax.axis_index("b"), lax.axis_index("rep")
    size = part_in.shape[1]
    width = weights.shape[2]
    first, second, last = members(own)
    weights[own] = stay[...]
    weights[first] = whole[...]
    weights[second] = theirs[:, :width]
    weights[last, :, half_of(rep, size)] = part_in[...]
    weights[last, :, half_of(1 - rep, size)] = theirs[:, width:]
    units = weights.shape[1] // 3
    model = weights.shape[2]
    far, _, piece, _ = part.shape
    both = [None] * 2
    for b in range(weights.shape[0]):
        rows = panel_of(panel, b)
        first = dot(weights[b, : 2 * units, :], rows[:, :model], FLIPPED)
        last = dot(weights[b, 2 * units :, :], rows[:, model:], FLIPPED)
        both = [first, last] if b == 0 else [both[0] + first, both[1] + last]
    for a in range(far):
        part[a, 0] = both[0][a * piece : (a + 1) * piece].astype(BF16)
        part[a, 1] = both[0][units + a * piece : units + (a + 1) * piece].astype(BF16)
        part[a, 2] = both[1][a * piece : (a + 1) * piece].astype(BF16)


def pointwise_body(parts, out):
    total = parts[0].astype(F32)
    for a in range(1, parts.shape[0]):
        total = total + parts[a].astype(F32)
    gate, up, back = total[0], total[1], total[2]
    sig = jax.nn.sigmoid(gate)
    out[0] = (gate * sig * up).astype(BF16)
    out[1] = (back * up * sig * (1.0 + gate * (1.0 - sig))).astype(BF16)
    out[2] = (back * gate * sig).astype(BF16)


def assemble(mid, place):
    return jnp.concatenate([mid[a, place].astype(F32) for a in range(mid.shape[0])], axis=0)


def outputs_body(mid, weights, out):
    units = weights.shape[1] // 3
    model = weights.shape[2]
    cols, near, block, _ = out.shape
    hidden, gate, up = (assemble(mid, m).T.astype(BF16) for m in range(3))
    for b in range(near):
        ahead = dot(hidden, weights[b, 2 * units :, :], PLAIN)
        behind = dot(gate, weights[b, :units, :], PLAIN) + dot(up, weights[b, units : 2 * units, :], PLAIN)
        out[:, b, :, :model] = ahead.astype(BF16).reshape(cols, block, model)
        out[:, b, :, model:] = behind.astype(BF16).reshape(cols, block, model)


def terms_body(marked, panel, other_panel, mid, other_mid, stay, whole, part, full):
    own, rep = lax.axis_index("b"), lax.axis_index("rep")
    first, _, last = members(own)
    cols, _, block, double = panel.shape
    model = double // 2
    size = part.shape[1]
    units = stay.shape[0] // 3
    sources = [
        (rows, *(assemble(values, m).astype(BF16) for m in range(3)))
        for rows, values in ((panel, mid), (other_panel, other_mid))
    ]

    for member, out in ((own, stay), (first, whole), (last, full)):
        total = [0.0, 0.0, 0.0]
        for rows, hidden, gate, up in sources:
            block_rows = rows[:, member].reshape(cols * block, double)
            total[0] = total[0] + dot(gate, block_rows[:, :model], PLAIN)
            total[1] = total[1] + dot(up, block_rows[:, :model], PLAIN)
            total[2] = total[2] + dot(hidden, block_rows[:, model:], PLAIN)
        for place in range(3):
            out[place * units : (place + 1) * units, :] = total[place].astype(BF16)
    part[...] = full[:, half_of(rep, size)]


def fold_body(pieces, out):
    total = pieces[0].astype(F32)
    for c in range(1, pieces.shape[0]):
        total = total + pieces[c].astype(F32)
    out[...] = total.astype(BF16)


def finish_body(pieces, mixed, input_grad):
    model = mixed.shape[1]
    total = pieces[0].astype(F32)
    for b in range(1, pieces.shape[0]):
        total = total + pieces[b].astype(F32)
    mixed[...] = total[:, :model].astype(BF16)
    input_grad[...] = total[:, model:].astype(BF16)


def unpack_body(
    marked,
    stay,
    whole,
    part,
    theirs,
    gate_keep,
    up_keep,
    down_keep,
    gate_out,
    up_out,
    down_out,
    pieces,
    tall,
):
    own, rep = lax.axis_index("b"), lax.axis_index("rep")
    first, second, last = members(own)
    size = part.shape[1]
    model = stay.shape[1]
    units = stay.shape[0] // 3
    blocks = gate_keep.shape[1]
    span = gate_out.shape[1] // blocks

    pieces[own] = stay[...]
    pieces[first] = whole[...]
    pieces[second] = theirs[:, :model]
    pieces[last, :, half_of(rep, size)] = part[...]
    pieces[last, :, half_of(1 - rep, size)] = theirs[:, model:]
    for place, keep, out in ((0, gate_keep, gate_out), (1, up_keep, up_out), (2, down_keep, down_out)):
        for member in range(pieces.shape[0]):
            tall[member * units : (member + 1) * units, :] = pieces[
                member, place * units : (place + 1) * units, :
            ]
        turned = tall[...].T if place < 2 else None
        for h in range(HALVES):
            for b in range(blocks):
                if place < 2:
                    at = (slice(h * size, (h + 1) * size), slice(b * span, (b + 1) * span))
                    out[at] = pick(keep[h, b], turned[at])
                else:
                    at = (slice(b * span, (b + 1) * span), slice(h * size, (h + 1) * size))
                    out[at] = pick(keep[h, b], tall[at])


def spread(value, axis):
    count = lax.axis_size(axis)
    return lax.all_to_all(jnp.broadcast_to(value[None], (count,) + value.shape), axis, 0, 0)


def exchange(whole, part, group):
    whole_moves = [
        (HALVES * b + r, HALVES * (b ^ (1 + r)) + r) for b in range(group) for r in range(HALVES)
    ]
    whole = lax.ppermute(whole, ("b", "rep"), whole_moves)
    part = lax.ppermute(part, "b", [(b, b ^ 3) for b in range(group)])
    return whole, part


def per_device(tokens, grad_out, gate_weight, up_weight, down_weight, gate_keep, up_keep, down_keep):
    far = lax.axis_size("a")
    group = lax.axis_size("b")
    cols = lax.axis_size("col")
    block, model = tokens.shape
    width = gate_weight.shape[1]
    units = width // group
    piece = units // far
    held = cols * block
    size = model // HALVES
    down_keep = down_keep.T
    panel = spread(jnp.concatenate([tokens, grad_out], axis=1), "b")
    stay, whole, part = call(
        prepare_body,
        [VMEM] * 3 + [SMEM] * 3,
        [local(3 * units, model)] * 2 + [local(3 * units, size)],
        [
            pltpu.VMEM((group, 3 * units, model), BF16),
            pltpu.VMEM((model, width), BF16),
            pltpu.VMEM((width, model), BF16),
        ],
    )(*map(distant, (gate_weight, up_weight, down_weight, gate_keep, up_keep, down_keep)))
    whole, part = exchange(whole, part, group)
    panel = near(spread(panel, "col"))
    (packed,) = call(pack_body, [VMEM] * 2, [local(3 * units, model + size)])(
        near(whole), near(part)
    )
    theirs = lax.ppermute(packed, "rep", SWAP)
    (first_mark,) = call(mark_body, [], [local(16, 128)])()
    weights, partial = call(
        partial_body,
        [VMEM] * 6,
        [outside(group, 3 * units, model), local(far, 3, piece, held)],
    )(first_mark, panel, stay, near(whole), near(part), near(theirs))
    parts = lax.all_to_all(partial, "a", 0, 0)
    other_panel = lax.ppermute(panel, "rep", SWAP)
    (second_mark,) = call(next_mark_body, [VMEM], [local(16, 128)])(first_mark)
    (own,) = call(pointwise_body, [VMEM], [local(3, piece, held)])(near(parts))
    mid = lax.all_gather(own.reshape(3 * piece, held), "a", axis=0, tiled=True)
    mid = near(mid.reshape(far, 3, piece, held))
    (out,) = call(outputs_body, [VMEM] * 2, [local(cols, group, block, 2 * model)])(
        mid, distant(weights)
    )
    pieces = lax.all_to_all(out, "col", 0, 0)
    other_mid = lax.ppermute(mid, "rep", SWAP)
    stay, whole, part = call(
        terms_body,
        [VMEM] * 5,
        [outside(3 * units, model), local(3 * units, model), local(3 * units, size)],
        [pltpu.VMEM((3 * units, model), BF16)],
    )(second_mark, panel, near(other_panel), mid, near(other_mid))
    whole, part = exchange(whole, part, group)
    (third_mark,) = call(next_mark_body, [VMEM], [local(16, 128)])(second_mark)
    (folded,) = call(fold_body, [VMEM], [local(group, block, 2 * model)])(near(pieces))
    last = lax.all_to_all(folded, "b", 0, 0)
    (packed,) = call(pack_body, [VMEM] * 2, [local(3 * units, model + size)])(
        near(whole), near(part)
    )
    theirs = lax.ppermute(packed, "rep", SWAP)
    mixed, input_grad = call(finish_body, [VMEM], [shape(block, model)] * 2)(near(last))
    gate_grad, up_grad, down_grad = call(
        unpack_body,
        [VMEM] * 5 + [SMEM] * 3,
        [shape(model, width), shape(model, width), shape(width, model)],
        [pltpu.VMEM((group, 3 * units, model), BF16), pltpu.VMEM((width, model), BF16)],
    )(
        third_mark,
        distant(stay),
        near(whole),
        near(part),
        near(theirs),
        *map(distant, (gate_keep, up_keep, down_keep)),
    )
    return (mixed, input_grad, gate_grad, up_grad, down_grad)


def solution(mesh):
    rows = mesh.shape["row"]
    grid = Mesh(
        mesh.devices.reshape(rows // NEAR, NEAR, mesh.shape["col"], mesh.shape["rep"]),
        ("a", "b", "col", "rep"),
    )
    row = ("a", "b")
    return jax.shard_map(
        per_device,
        mesh=grid,
        in_specs=(
            P(("col", "rep"), row),
            P(("col", "rep"), row),
            P(row, "col"),
            P(row, "col"),
            P("col", row),
            P(row, "col"),
            P(row, "col"),
            P("col", row),
        ),
        out_specs=(
            P(("col", "rep"), row),
            P(("col", "rep"), row),
            P(row, "col"),
            P(row, "col"),
            P("col", row),
        ),
        check_vma=False,
    )
```

```python
import jax
import jax.numpy as jnp
from jax import lax
from jax.experimental import pallas as pl
from jax.experimental.pallas import tpu as pltpu
from jax.sharding import Mesh, PartitionSpec as P


BF16 = jnp.bfloat16
F32 = jnp.float32
PLAIN = (((1,), (0,)), ((), ()))
FLIPPED = (((1,), (1,)), ((), ()))
NEAR = 4
LIMIT = 16 * 1024 * 1024
HALVES = 2
SWAP = [(0, 1), (1, 0)]
VMEM = pl.BlockSpec(memory_space=pltpu.VMEM)
SMEM = pl.BlockSpec(memory_space=pltpu.SMEM)


def dot(left, right, dims):
    return lax.dot_general(left, right, dims, preferred_element_type=F32)


def shape(*dims):
    return jax.ShapeDtypeStruct(dims, BF16)


def call(body, ins, outs, scratch=()):
    return pl.pallas_call(
        body,
        in_specs=ins,
        out_specs=[VMEM] * len(outs),
        out_shape=list(outs),
        scratch_shapes=list(scratch),
        compiler_params=pltpu.CompilerParams(vmem_limit_bytes=LIMIT),
    )


def near(value):
    return pltpu.with_memory_space_constraint(value, pltpu.VMEM)


def local(*dims):
    return pltpu.VMEM(dims, BF16)


def outside(*dims):
    return pltpu.HBM(dims, BF16)


def mark_body(out):
    out[...] = jnp.zeros_like(out)


def next_mark_body(before, out):
    out[...] = before[...]


def distant(value):
    return pltpu.with_memory_space_constraint(value, pltpu.HBM)


def half_of(index, size):
    return pl.ds(pl.multiple_of(index * size, size), size)


def pick(keep, value):
    return jnp.where(keep != 0, value, jnp.zeros_like(value))


def members(own):
    rep = lax.axis_index("rep")
    return own ^ (1 + rep), own ^ (2 - rep), own ^ 3


def prepare_body(gate, up, down, gate_keep, up_keep, down_keep, stay, whole, part, full, rows, tall):
    own, rep = lax.axis_index("b"), lax.axis_index("rep")
    blocks = gate_keep.shape[1]
    span = gate.shape[1] // blocks
    size = part.shape[1]
    units = stay.shape[0] // 3
    for place, source, keep in ((0, gate, gate_keep), (1, up, up_keep)):
        for h in range(HALVES):
            for b in range(blocks):
                cut = (slice(h * size, (h + 1) * size), slice(b * span, (b + 1) * span))
                rows[cut] = pick(keep[h, b], source[cut])
        turned = rows[...].T
        for b in range(full.shape[0]):
            full[b, place * units : (place + 1) * units, :] = turned[b * units : (b + 1) * units]
    for h in range(HALVES):
        for b in range(blocks):
            cut = (slice(b * span, (b + 1) * span), slice(h * size, (h + 1) * size))
            tall[cut] = pick(down_keep[h, b], down[cut])
    for b in range(full.shape[0]):
        full[b, 2 * units : 3 * units, :] = tall[b * units : (b + 1) * units, :]
    first, _, last = members(own)
    stay[...] = full[own]
    whole[...] = full[first]
    part[...] = full[last, :, half_of(rep, size)]


def pack_body(whole, part, out):
    width = whole.shape[1]
    out[:, :width] = whole[...]
    out[:, width:] = part[...]


def panel_of(panel, b):
    cols, _, block, width = panel.shape
    return panel[:, b].reshape(cols * block, width)


def partial_body(marked, panel, stay, whole, part_in, theirs, weights, part):
    own, rep = lax.axis_index("b"), lax.axis_index("rep")
    size = part_in.shape[1]
    width = weights.shape[2]
    first, second, last = members(own)
    weights[own] = stay[...]
    weights[first] = whole[...]
    weights[second] = theirs[:, :width]
    weights[last, :, half_of(rep, size)] = part_in[...]
    weights[last, :, half_of(1 - rep, size)] = theirs[:, width:]
    units = weights.shape[1] // 3
    model = weights.shape[2]
    far, _, piece, _ = part.shape
    both = [None] * 2
    for b in range(weights.shape[0]):
        rows = panel_of(panel, b)
        first = dot(weights[b, : 2 * units, :], rows[:, :model], FLIPPED)
        last = dot(weights[b, 2 * units :, :], rows[:, model:], FLIPPED)
        both = [first, last] if b == 0 else [both[0] + first, both[1] + last]
    for a in range(far):
        part[a, 0] = both[0][a * piece : (a + 1) * piece].astype(BF16)
        part[a, 1] = both[0][units + a * piece : units + (a + 1) * piece].astype(BF16)
        part[a, 2] = both[1][a * piece : (a + 1) * piece].astype(BF16)


def pointwise_body(parts, out):
    total = parts[0].astype(F32)
    for a in range(1, parts.shape[0]):
        total = total + parts[a].astype(F32)
    gate, up, back = total[0], total[1], total[2]
    sig = jax.nn.sigmoid(gate)
    out[0] = (gate * sig * up).astype(BF16)
    out[1] = (back * up * sig * (1.0 + gate * (1.0 - sig))).astype(BF16)
    out[2] = (back * gate * sig).astype(BF16)


def assemble(mid, place):
    return jnp.concatenate([mid[a, place].astype(F32) for a in range(mid.shape[0])], axis=0)


def outputs_body(mid, weights, out):
    units = weights.shape[1] // 3
    model = weights.shape[2]
    cols, near, block, _ = out.shape
    hidden, gate, up = (assemble(mid, m).T.astype(BF16) for m in range(3))
    for b in range(near):
        ahead = dot(hidden, weights[b, 2 * units :, :], PLAIN)
        behind = dot(gate, weights[b, :units, :], PLAIN) + dot(up, weights[b, units : 2 * units, :], PLAIN)
        out[:, b, :, :model] = ahead.astype(BF16).reshape(cols, block, model)
        out[:, b, :, model:] = behind.astype(BF16).reshape(cols, block, model)


def terms_body(marked, panel, other_panel, mid, other_mid, stay, whole, part, full):
    own, rep = lax.axis_index("b"), lax.axis_index("rep")
    first, _, last = members(own)
    cols, _, block, double = panel.shape
    model = double // 2
    size = part.shape[1]
    units = stay.shape[0] // 3
    sources = [
        (rows, *(assemble(values, m).astype(BF16) for m in range(3)))
        for rows, values in ((panel, mid), (other_panel, other_mid))
    ]

    for member, out in ((own, stay), (first, whole), (last, full)):
        total = [0.0, 0.0, 0.0]
        for rows, hidden, gate, up in sources:
            block_rows = rows[:, member].reshape(cols * block, double)
            total[0] = total[0] + dot(gate, block_rows[:, :model], PLAIN)
            total[1] = total[1] + dot(up, block_rows[:, :model], PLAIN)
            total[2] = total[2] + dot(hidden, block_rows[:, model:], PLAIN)
        for place in range(3):
            out[place * units : (place + 1) * units, :] = total[place].astype(BF16)
    part[...] = full[:, half_of(rep, size)]


def fold_body(pieces, out):
    total = pieces[0].astype(F32)
    for c in range(1, pieces.shape[0]):
        total = total + pieces[c].astype(F32)
    out[...] = total.astype(BF16)


def finish_body(pieces, mixed, input_grad):
    model = mixed.shape[1]
    total = pieces[0].astype(F32)
    for b in range(1, pieces.shape[0]):
        total = total + pieces[b].astype(F32)
    mixed[...] = total[:, :model].astype(BF16)
    input_grad[...] = total[:, model:].astype(BF16)


def unpack_body(
    marked,
    stay,
    whole,
    part,
    theirs,
    gate_keep,
    up_keep,
    down_keep,
    gate_out,
    up_out,
    down_out,
    pieces,
):
    own, rep = lax.axis_index("b"), lax.axis_index("rep")
    first, second, last = members(own)
    size = part.shape[1]
    model = stay.shape[1]
    units = stay.shape[0] // 3
    blocks = gate_keep.shape[1]
    span = gate_out.shape[1] // blocks

    for place, keep, out in ((0, gate_keep, gate_out), (1, up_keep, up_out), (2, down_keep, down_out)):
        cut = slice(place * units, (place + 1) * units)
        pieces[place, own] = stay[cut, :]
        pieces[place, first] = whole[cut, :]
        pieces[place, second] = theirs[cut, :model]
        pieces[place, last, :, half_of(rep, size)] = part[cut, :]
        pieces[place, last, :, half_of(1 - rep, size)] = theirs[cut, model:]
        value = pieces[place].reshape(pieces.shape[1] * units, model)
        if place < 2:
            value = value.T
        for h in range(HALVES):
            for b in range(blocks):
                at = (slice(h * size, (h + 1) * size), slice(b * span, (b + 1) * span))
                at = at if place < 2 else at[::-1]
                out[at] = pick(keep[h, b], value[at])


def spread(value, axis):
    count = lax.axis_size(axis)
    return lax.all_to_all(jnp.broadcast_to(value[None], (count,) + value.shape), axis, 0, 0)


def exchange(whole, part, group):
    whole_moves = [
        (HALVES * b + r, HALVES * (b ^ (1 + r)) + r) for b in range(group) for r in range(HALVES)
    ]
    whole = lax.ppermute(whole, ("b", "rep"), whole_moves)
    part = lax.ppermute(part, "b", [(b, b ^ 3) for b in range(group)])
    return whole, part


def per_device(tokens, grad_out, gate_weight, up_weight, down_weight, gate_keep, up_keep, down_keep):
    far = lax.axis_size("a")
    group = lax.axis_size("b")
    cols = lax.axis_size("col")
    block, model = tokens.shape
    width = gate_weight.shape[1]
    units = width // group
    piece = units // far
    held = cols * block
    size = model // HALVES
    down_keep = down_keep.T
    panel = spread(jnp.concatenate([tokens, grad_out], axis=1), "b")
    stay, whole, part = call(
        prepare_body,
        [VMEM] * 3 + [SMEM] * 3,
        [local(3 * units, model)] * 2 + [local(3 * units, size)],
        [
            pltpu.VMEM((group, 3 * units, model), BF16),
            pltpu.VMEM((model, width), BF16),
            pltpu.VMEM((width, model), BF16),
        ],
    )(*map(distant, (gate_weight, up_weight, down_weight, gate_keep, up_keep, down_keep)))
    whole, part = exchange(whole, part, group)
    panel = near(spread(panel, "col"))
    (packed,) = call(pack_body, [VMEM] * 2, [local(3 * units, model + size)])(
        near(whole), near(part)
    )
    theirs = lax.ppermute(packed, "rep", SWAP)
    (first_mark,) = call(mark_body, [], [local(16, 128)])()
    weights, partial = call(
        partial_body,
        [VMEM] * 6,
        [outside(group, 3 * units, model), local(far, 3, piece, held)],
    )(first_mark, panel, stay, near(whole), near(part), near(theirs))
    parts = lax.all_to_all(partial, "a", 0, 0)
    other_panel = lax.ppermute(panel, "rep", SWAP)
    (second_mark,) = call(next_mark_body, [VMEM], [local(16, 128)])(first_mark)
    (own,) = call(pointwise_body, [VMEM], [local(3, piece, held)])(near(parts))
    mid = lax.all_gather(own.reshape(3 * piece, held), "a", axis=0, tiled=True)
    mid = near(mid.reshape(far, 3, piece, held))
    (out,) = call(outputs_body, [VMEM] * 2, [local(cols, group, block, 2 * model)])(
        mid, distant(weights)
    )
    pieces = lax.all_to_all(out, "col", 0, 0)
    other_mid = lax.ppermute(mid, "rep", SWAP)
    stay, whole, part = call(
        terms_body,
        [VMEM] * 5,
        [outside(3 * units, model), local(3 * units, model), local(3 * units, size)],
        [pltpu.VMEM((3 * units, model), BF16)],
    )(second_mark, panel, near(other_panel), mid, near(other_mid))
    whole, part = exchange(whole, part, group)
    (third_mark,) = call(next_mark_body, [VMEM], [local(16, 128)])(second_mark)
    (folded,) = call(fold_body, [VMEM], [local(group, block, 2 * model)])(near(pieces))
    last = lax.all_to_all(folded, "b", 0, 0)
    (packed,) = call(pack_body, [VMEM] * 2, [local(3 * units, model + size)])(
        near(whole), near(part)
    )
    theirs = lax.ppermute(packed, "rep", SWAP)
    mixed, input_grad = call(finish_body, [VMEM], [shape(block, model)] * 2)(near(last))
    gate_grad, up_grad, down_grad = call(
        unpack_body,
        [VMEM] * 5 + [SMEM] * 3,
        [shape(model, width), shape(model, width), shape(width, model)],
        [pltpu.VMEM((3, group, units, model), BF16)],
    )(
        third_mark,
        distant(stay),
        near(whole),
        near(part),
        near(theirs),
        *map(distant, (gate_keep, up_keep, down_keep)),
    )
    return (mixed, input_grad, gate_grad, up_grad, down_grad)


def solution(mesh):
    rows = mesh.shape["row"]
    grid = Mesh(
        mesh.devices.reshape(rows // NEAR, NEAR, mesh.shape["col"], mesh.shape["rep"]),
        ("a", "b", "col", "rep"),
    )
    row = ("a", "b")
    return jax.shard_map(
        per_device,
        mesh=grid,
        in_specs=(
            P(("col", "rep"), row),
            P(("col", "rep"), row),
            P(row, "col"),
            P(row, "col"),
            P("col", row),
            P(row, "col"),
            P(row, "col"),
            P("col", row),
        ),
        out_specs=(
            P(("col", "rep"), row),
            P(("col", "rep"), row),
            P(row, "col"),
            P(row, "col"),
            P("col", row),
        ),
        check_vma=False,
    )
```

```python
import jax
import jax.numpy as jnp
from jax import lax
from jax.experimental import pallas as pl
from jax.experimental.pallas import tpu as pltpu
from jax.sharding import Mesh, PartitionSpec as P


BF16 = jnp.bfloat16
F32 = jnp.float32
PLAIN = (((1,), (0,)), ((), ()))
FLIPPED = (((1,), (1,)), ((), ()))
NEAR = 4
LIMIT = 16 * 1024 * 1024
HALVES = 2
SWAP = [(0, 1), (1, 0)]
VMEM = pl.BlockSpec(memory_space=pltpu.VMEM)
SMEM = pl.BlockSpec(memory_space=pltpu.SMEM)


def dot(left, right, dims):
    return lax.dot_general(left, right, dims, preferred_element_type=F32)


def shape(*dims):
    return jax.ShapeDtypeStruct(dims, BF16)


def call(body, ins, outs, scratch=()):
    return pl.pallas_call(
        body,
        in_specs=ins,
        out_specs=[VMEM] * len(outs),
        out_shape=list(outs),
        scratch_shapes=list(scratch),
        compiler_params=pltpu.CompilerParams(vmem_limit_bytes=LIMIT),
    )


def near(value):
    return pltpu.with_memory_space_constraint(value, pltpu.VMEM)


def local(*dims):
    return pltpu.VMEM(dims, BF16)


def outside(*dims):
    return pltpu.HBM(dims, BF16)


def mark_body(out):
    out[...] = jnp.zeros_like(out)


def next_mark_body(before, out):
    out[...] = before[...]


def distant(value):
    return pltpu.with_memory_space_constraint(value, pltpu.HBM)


def half_of(index, size):
    return pl.ds(pl.multiple_of(index * size, size), size)


def pick(keep, value):
    return jnp.where(keep != 0, value, jnp.zeros_like(value))


def members(own):
    rep = lax.axis_index("rep")
    return own ^ (1 + rep), own ^ (2 - rep), own ^ 3


def prepare_body(gate, up, down, gate_keep, up_keep, down_keep, stay, whole, part, full, rows, tall):
    own, rep = lax.axis_index("b"), lax.axis_index("rep")
    blocks = gate_keep.shape[1]
    span = gate.shape[1] // blocks
    size = part.shape[1]
    units = stay.shape[0] // 3
    for place, source, keep in ((0, gate, gate_keep), (1, up, up_keep)):
        for h in range(HALVES):
            for b in range(blocks):
                cut = (slice(h * size, (h + 1) * size), slice(b * span, (b + 1) * span))
                rows[cut] = pick(keep[h, b], source[cut])
        turned = rows[...].T
        for b in range(full.shape[0]):
            full[b, place * units : (place + 1) * units, :] = turned[b * units : (b + 1) * units]
    for h in range(HALVES):
        for b in range(blocks):
            cut = (slice(b * span, (b + 1) * span), slice(h * size, (h + 1) * size))
            tall[cut] = pick(down_keep[h, b], down[cut])
    for b in range(full.shape[0]):
        full[b, 2 * units : 3 * units, :] = tall[b * units : (b + 1) * units, :]
    first, _, last = members(own)
    stay[...] = full[own]
    whole[...] = full[first]
    part[...] = full[last, :, half_of(rep, size)]


def pack_body(whole, part, out):
    width = whole.shape[1]
    out[:, :width] = whole[...]
    out[:, width:] = part[...]


def panel_of(panel, b):
    cols, _, block, width = panel.shape
    return panel[:, b].reshape(cols * block, width)


def partial_body(marked, panel, stay, whole, part_in, theirs, weights, part):
    own, rep = lax.axis_index("b"), lax.axis_index("rep")
    size = part_in.shape[1]
    width = weights.shape[2]
    first, second, last = members(own)
    weights[own] = stay[...]
    weights[first] = whole[...]
    weights[second] = theirs[:, :width]
    weights[last, :, half_of(rep, size)] = part_in[...]
    weights[last, :, half_of(1 - rep, size)] = theirs[:, width:]
    units = weights.shape[1] // 3
    model = weights.shape[2]
    far, _, piece, _ = part.shape
    both = [None] * 2
    for b in range(weights.shape[0]):
        rows = panel_of(panel, b)
        first = dot(weights[b, : 2 * units, :], rows[:, :model], FLIPPED)
        last = dot(weights[b, 2 * units :, :], rows[:, model:], FLIPPED)
        both = [first, last] if b == 0 else [both[0] + first, both[1] + last]
    for a in range(far):
        part[a, 0] = both[0][a * piece : (a + 1) * piece].astype(BF16)
        part[a, 1] = both[0][units + a * piece : units + (a + 1) * piece].astype(BF16)
        part[a, 2] = both[1][a * piece : (a + 1) * piece].astype(BF16)


def pointwise_body(parts, out):
    total = parts[0].astype(F32)
    for a in range(1, parts.shape[0]):
        total = total + parts[a].astype(F32)
    gate, up, back = total[0], total[1], total[2]
    sig = jax.nn.sigmoid(gate)
    out[0] = (gate * sig * up).astype(BF16)
    out[1] = (back * up * sig * (1.0 + gate * (1.0 - sig))).astype(BF16)
    out[2] = (back * gate * sig).astype(BF16)


def assemble(mid, place):
    return jnp.concatenate([mid[a, place].astype(F32) for a in range(mid.shape[0])], axis=0)


def outputs_body(mid, weights, out):
    units = weights.shape[1] // 3
    model = weights.shape[2]
    cols, near, block, _ = out.shape
    hidden, gate, up = (assemble(mid, m).T.astype(BF16) for m in range(3))
    for b in range(near):
        ahead = dot(hidden, weights[b, 2 * units :, :], PLAIN)
        behind = dot(gate, weights[b, :units, :], PLAIN) + dot(up, weights[b, units : 2 * units, :], PLAIN)
        out[:, b, :, :model] = ahead.astype(BF16).reshape(cols, block, model)
        out[:, b, :, model:] = behind.astype(BF16).reshape(cols, block, model)


def terms_body(marked, panel, other_panel, mid, other_mid, stay, whole, part, full):
    own, rep = lax.axis_index("b"), lax.axis_index("rep")
    first, _, last = members(own)
    cols, _, block, double = panel.shape
    model = double // 2
    size = part.shape[1]
    units = stay.shape[0] // 3
    sources = [
        (rows, *(assemble(values, m).astype(BF16) for m in range(3)))
        for rows, values in ((panel, mid), (other_panel, other_mid))
    ]

    for member, out in ((own, stay), (first, whole), (last, full)):
        total = [0.0, 0.0, 0.0]
        for rows, hidden, gate, up in sources:
            block_rows = rows[:, member].reshape(cols * block, double)
            total[0] = total[0] + dot(gate, block_rows[:, :model], PLAIN)
            total[1] = total[1] + dot(up, block_rows[:, :model], PLAIN)
            total[2] = total[2] + dot(hidden, block_rows[:, model:], PLAIN)
        for place in range(3):
            out[place * units : (place + 1) * units, :] = total[place].astype(BF16)
    part[...] = full[:, half_of(rep, size)]


def fold_body(pieces, out):
    total = pieces[0].astype(F32)
    for c in range(1, pieces.shape[0]):
        total = total + pieces[c].astype(F32)
    out[...] = total.astype(BF16)


def finish_body(pieces, mixed, input_grad):
    model = mixed.shape[1]
    total = pieces[0].astype(F32)
    for b in range(1, pieces.shape[0]):
        total = total + pieces[b].astype(F32)
    mixed[...] = total[:, :model].astype(BF16)
    input_grad[...] = total[:, model:].astype(BF16)


def unpack_body(
    marked,
    stay,
    whole,
    part,
    theirs,
    gate_keep,
    up_keep,
    down_keep,
    gate_out,
    up_out,
    down_out,
    pieces,
):
    own, rep = lax.axis_index("b"), lax.axis_index("rep")
    first, second, last = members(own)
    size = part.shape[1]
    model = stay.shape[1]
    units = stay.shape[0] // 3
    blocks = gate_keep.shape[1]
    span = gate_out.shape[1] // blocks

    for place, keep, out in ((0, gate_keep, gate_out), (1, up_keep, up_out), (2, down_keep, down_out)):
        cut = slice(place * units, (place + 1) * units)
        pieces[place, own] = stay[cut, :]
        pieces[place, first] = whole[cut, :]
        pieces[place, second] = theirs[cut, :model]
        pieces[place, last, :, half_of(rep, size)] = part[cut, :]
        pieces[place, last, :, half_of(1 - rep, size)] = theirs[cut, model:]
        value = pieces[place].reshape(pieces.shape[1] * units, model)
        if place < 2:
            value = value.T
        for h in range(HALVES):
            for b in range(blocks):
                at = (slice(h * size, (h + 1) * size), slice(b * span, (b + 1) * span))
                at = at if place < 2 else at[::-1]
                out[at] = pick(keep[h, b], value[at])


def spread(value, axis):
    count = lax.axis_size(axis)
    return lax.all_to_all(jnp.broadcast_to(value[None], (count,) + value.shape), axis, 0, 0)


def exchange(whole, part, group):
    whole_moves = [
        (HALVES * b + r, HALVES * (b ^ (1 + r)) + r) for b in range(group) for r in range(HALVES)
    ]
    whole = lax.ppermute(whole, ("b", "rep"), whole_moves)
    part = lax.ppermute(part, "b", [(b, b ^ 3) for b in range(group)])
    return whole, part


def per_device(tokens, grad_out, gate_weight, up_weight, down_weight, gate_keep, up_keep, down_keep):
    far = lax.axis_size("a")
    group = lax.axis_size("b")
    cols = lax.axis_size("col")
    block, model = tokens.shape
    width = gate_weight.shape[1]
    units = width // group
    piece = units // far
    held = cols * block
    size = model // HALVES
    down_keep = down_keep.T
    panel = spread(jnp.concatenate([tokens, grad_out], axis=1), "b")
    stay, whole, part = call(
        prepare_body,
        [VMEM] * 3 + [SMEM] * 3,
        [local(3 * units, model)] * 2 + [local(3 * units, size)],
        [
            pltpu.VMEM((group, 3 * units, model), BF16),
            pltpu.VMEM((model, width), BF16),
            pltpu.VMEM((width, model), BF16),
        ],
    )(*map(distant, (gate_weight, up_weight, down_weight, gate_keep, up_keep, down_keep)))
    whole, part = exchange(whole, part, group)
    panel = near(spread(panel, "col"))
    (packed,) = call(pack_body, [VMEM] * 2, [local(3 * units, model + size)])(
        near(whole), near(part)
    )
    theirs = lax.ppermute(packed, "rep", SWAP)
    (first_mark,) = call(mark_body, [], [local(16, 128)])()
    weights, partial = call(
        partial_body,
        [VMEM] * 6,
        [local(group, 3 * units, model), local(far, 3, piece, held)],
    )(first_mark, panel, stay, near(whole), near(part), near(theirs))
    parts = lax.all_to_all(partial, "a", 0, 0)
    other_panel = lax.ppermute(panel, "rep", SWAP)
    (second_mark,) = call(next_mark_body, [VMEM], [local(16, 128)])(first_mark)
    (own,) = call(pointwise_body, [VMEM], [local(3, piece, held)])(near(parts))
    mid = lax.all_gather(own.reshape(3 * piece, held), "a", axis=0, tiled=True)
    mid = near(mid.reshape(far, 3, piece, held))
    (out,) = call(outputs_body, [VMEM] * 2, [local(cols, group, block, 2 * model)])(mid, weights)
    pieces = lax.all_to_all(out, "col", 0, 0)
    other_mid = lax.ppermute(mid, "rep", SWAP)
    stay, whole, part = call(
        terms_body,
        [VMEM] * 5,
        [outside(3 * units, model), local(3 * units, model), local(3 * units, size)],
        [pltpu.VMEM((3 * units, model), BF16)],
    )(second_mark, panel, near(other_panel), mid, near(other_mid))
    whole, part = exchange(whole, part, group)
    (third_mark,) = call(next_mark_body, [VMEM], [local(16, 128)])(second_mark)
    (folded,) = call(fold_body, [VMEM], [local(group, block, 2 * model)])(near(pieces))
    last = lax.all_to_all(folded, "b", 0, 0)
    (packed,) = call(pack_body, [VMEM] * 2, [local(3 * units, model + size)])(
        near(whole), near(part)
    )
    theirs = lax.ppermute(packed, "rep", SWAP)
    mixed, input_grad = call(finish_body, [VMEM], [shape(block, model)] * 2)(near(last))
    gate_grad, up_grad, down_grad = call(
        unpack_body,
        [VMEM] * 5 + [SMEM] * 3,
        [shape(model, width), shape(model, width), shape(width, model)],
        [pltpu.VMEM((3, group, units, model), BF16)],
    )(
        third_mark,
        distant(stay),
        near(whole),
        near(part),
        near(theirs),
        *map(distant, (gate_keep, up_keep, down_keep)),
    )
    return (mixed, input_grad, gate_grad, up_grad, down_grad)


def solution(mesh):
    rows = mesh.shape["row"]
    grid = Mesh(
        mesh.devices.reshape(rows // NEAR, NEAR, mesh.shape["col"], mesh.shape["rep"]),
        ("a", "b", "col", "rep"),
    )
    row = ("a", "b")
    return jax.shard_map(
        per_device,
        mesh=grid,
        in_specs=(
            P(("col", "rep"), row),
            P(("col", "rep"), row),
            P(row, "col"),
            P(row, "col"),
            P("col", row),
            P(row, "col"),
            P(row, "col"),
            P("col", row),
        ),
        out_specs=(
            P(("col", "rep"), row),
            P(("col", "rep"), row),
            P(row, "col"),
            P(row, "col"),
            P("col", row),
        ),
        check_vma=False,
    )
```
